256 devices in a mesh: ctx: 16 (over z, core), head: 8 (over y, x_lo), dp: 2 (over x_hi).
Axes of the slice: x: 4 (x_hi: 2, x_lo: 2; x = x_hi * 2 + x_lo), y: 4, z: 8, core: 2. Of those that a mesh axis runs over, the one named last changes fastest.
Arguments:
- queries: bfloat16 [32768, 5120], P(('dp', 'ctx', 'head')), parts along dimension 0, may hold values from -64 to 64
- keys: bfloat16 [32768, 1024], P(('dp', 'ctx', 'head')), parts along dimension 0, may hold values from -4 to 4
- values: bfloat16 [32768, 1024], P(('dp', 'ctx', 'head')), parts along dimension 0, may hold values from -6 to 6
- doc_lengths: int32 [16], P('dp'), parts along dimension 0, may hold values from 1 to 9216, 16384 in all
- steering: float32 [5120], replicated, may hold values from -3 to 3
Outputs:
- steered: bfloat16 [32768, 5120], P(('dp', 'ctx', 'head')), parts along dimension 0
The draws below stay inside these ranges and needn't reach their ends.
There are 2 independent parts, one for each index of `dp`. The reference program is written for one: setup_inputs(seed, part) draws one part's arguments, and reference() takes and returns one part's arrays. A program takes and returns all parts, laid end to end along the dimension named above; an argument that names none is the same for every part. Nothing has to cross between parts.
Inputs may be any that keep to these rules, and one draw needn't show every extreme that they name: `doc_lengths`: the lengths sum to 16384.
All inputs are finite; a program needn't handle non-finite values.
Results may differ from the reference program's by a relative error of at most 0.0043.
Values may be sent and summed in bfloat16 or wider, within the bound.
No kernel may reach another device: no remote copies, remote signals or barrier semaphores. Data moves between devices by JAX's collectives and lax.ppermute only.
A program may use at most 64 MiB of HBM per device.

```python
import math
import jax
import jax.numpy as jnp
import numpy as np
from jax import lax

D = 5120
QH = 40
KVH = 8
HD = 128
NDOC = 8
TOKENS = 16384
MOST = 9216


def drawn_draw(key):
    root = jax.random.fold_in(key, 11)
    key_base = jax.random.fold_in(root, 0)
    key_query = jax.random.fold_in(root, 3)
    key_scale = jax.random.fold_in(root, 4)
    raw_keys = 3.0 * jax.random.truncated_normal(key_base, -4.0, 4.0, (TOKENS, KVH, HD), jnp.float32)
    key_vectors = jnp.clip(raw_keys, -4.0, 4.0)
    query_base = jax.random.truncated_normal(key_query, -4.0, 4.0, (TOKENS, QH * HD), jnp.float32)
    row_scales = jnp.exp(jax.random.uniform(key_scale, (TOKENS, 1), jnp.float32, math.log(0.5), math.log(5.0)))
    query_vectors = query_base * row_scales
    return (query_vectors, key_vectors.reshape(TOKENS, KVH * HD))


def draw_queries(key, part):
    return drawn_draw(key)[0].astype(jnp.bfloat16)


def draw_keys(key, part):
    return drawn_draw(key)[1].astype(jnp.bfloat16)


def steps_of(rng, shape, shards, low, high):
    level = 1.0
    for position, blocks in shards:
        steps = jax.random.uniform(jax.random.fold_in(jax.random.fold_in(rng, 6), position), (blocks,), jnp.float32, low / len(shards), high / len(shards))
        level = level * jnp.repeat(jnp.exp(steps), shape[position] // blocks).reshape((-1,) + (1,) * (len(shape) - 1 - position))
    return level


def length_profile(number_of, total, most, lean):
    loads = [(1 << 20) // math.isqrt(grade ** lean) + 1 for grade in range(2, number_of + 1)]
    rest, counts = total - most - (number_of - 1), [1] * (number_of - 1)
    while rest > 0:
        free = [i for i in range(number_of - 1) if counts[i] < most]
        pool, left = sum([loads[i] for i in free]), rest
        for i in free:
            more = min(most - counts[i], max(1, left * loads[i] // pool), rest)
            counts[i] = counts[i] + more
            rest = rest - more
    return np.array([most] + counts)


def ragged_sizes(rng, number_of, total, bound, lean):
    if number_of == 2:
        one = jax.random.randint(rng, (), max(1, total - bound), min(bound, total - 1) + 1)
        return jnp.stack([one, total - one])
    tallies = jnp.asarray(length_profile(number_of, total, bound, lean), jnp.int32)
    pairs = (number_of - 1) // 2
    source_of, receiver = tallies[1:1 + 2 * pairs:2], tallies[2:2 + 2 * pairs:2]
    margin = jnp.minimum(source_of - 1, bound - receiver)
    passed = jax.random.randint(jax.random.fold_in(rng, 1), (pairs,), 0, 1 << 20) % (margin + 1)
    tallies = tallies.at[1:1 + 2 * pairs:2].set(source_of - passed).at[2:2 + 2 * pairs:2].set(receiver + passed)
    return tallies[jax.random.permutation(jax.random.fold_in(rng, 2), number_of)]


def normal_values(stream_key, dims, scale, reach, cuts=(), kind=jnp.bfloat16):
    values = jax.random.normal(stream_key, dims, jnp.float32) * scale
    if len(cuts) > 0:
        values = steps_of(stream_key, dims, cuts, -0.22, 0.18) * values
    return jnp.clip(values, min=-reach, max=reach).astype(kind)


def setup_inputs(seed: int = 0, part: int = 0) -> dict:
    key_of = jax.random.split(jax.random.key(seed), 6)
    part_keys = jax.random.split(jax.random.fold_in(key_of[5], part), 6)
    queries = draw_queries(jax.random.fold_in(jax.random.fold_in(key_of[5], part), 71), part)
    keys = draw_keys(jax.random.fold_in(jax.random.fold_in(key_of[5], part), 71), part)
    values = normal_values(part_keys[2], (TOKENS, KVH * HD), 1.0, 6.0, ((0, 128),))
    doc_lengths = ragged_sizes(part_keys[3], NDOC, TOKENS, MOST, 2).astype(jnp.int32)
    steering = normal_values(key_of[4], (D,), 0.5, 3.0, (), jnp.float32)
    return {"queries": queries, "keys": keys, "values": values, "doc_lengths": doc_lengths, "steering": steering}


def doc_index(positions, bounds):
    return jnp.sum((positions[:, None] >= bounds[None, :]).astype(jnp.int32), axis=1)


def reference(queries, keys, values, doc_lengths, steering):
    groups = QH // KVH
    bounds = jnp.cumsum(doc_lengths).astype(jnp.int32)
    q_block = min(256, TOKENS)
    window = min(TOKENS, MOST + q_block)
    score_scale = HD ** -0.5
    query_heads = queries.reshape(TOKENS, KVH, groups, HD)
    key_heads = keys.reshape(TOKENS, KVH, HD)
    value_heads = values.reshape(TOKENS, KVH, HD)

    def one_block(block_index):
        q_start = (block_index * q_block).astype(jnp.int32)
        k_start = jnp.clip(q_start + q_block - window, 0, TOKENS - window).astype(jnp.int32)
        query_tile = lax.dynamic_slice_in_dim(query_heads, q_start, q_block, 0).astype(jnp.float32)
        key_tile = lax.dynamic_slice_in_dim(key_heads, k_start, window, 0).astype(jnp.float32)
        value_tile = lax.dynamic_slice_in_dim(value_heads, k_start, window, 0).astype(jnp.float32)
        q_positions = q_start + jnp.arange(q_block, dtype=jnp.int32)
        k_positions = k_start + jnp.arange(window, dtype=jnp.int32)
        q_docs = doc_index(q_positions, bounds)
        k_docs = doc_index(k_positions, bounds)
        visible = (q_docs[:, None] == k_docs[None, :]) & (k_positions[None, :] <= q_positions[:, None])
        visible = visible[:, None, None, :]
        scores = jnp.einsum('qhgd,khd->qhgk', query_tile, key_tile) * score_scale
        row_top = jnp.max(jnp.where(visible, scores, -jnp.inf), axis=3, keepdims=True)
        weights = jnp.where(visible, jnp.exp(scores - row_top), 0.0)
        denom = jnp.sum(weights, axis=3)
        rounded = lax.optimization_barrier(weights.astype(jnp.bfloat16)).astype(jnp.float32)
        mixed_out = jnp.einsum('qhgk,khd->qhgd', rounded, value_tile) / denom[..., None]
        return mixed_out.reshape(q_block, QH * HD).astype(jnp.bfloat16)

    attended = lax.map(one_block, jnp.arange(TOKENS // q_block, dtype=jnp.int32))
    attended = attended.reshape(TOKENS, QH * HD)
    return (attended.astype(jnp.float32) + steering[None, :]).astype(jnp.bfloat16)
```

```python
import functools
import math

import jax
import jax.numpy as jnp
from jax import lax
from jax.experimental import pallas as pl
from jax.experimental.pallas import tpu as pltpu
from jax.sharding import Mesh
from jax.sharding import PartitionSpec as P

QH = 40
KVH = 8
HD = 128
GROUPS = QH // KVH
NEG = -1e30
LOG2E = 1.4426950408889634
LAYERS = 8
PLANE = 8
SEG = 128
RUN = PLANE * SEG
KEY_TILE = 512


def attend_kernel(place, lengths, q_ref, kv_hbm, steer_ref, o_ref, kv, acc, top, sems):
    ndoc = lengths.shape[0]
    core = place[0]
    slot = place[1]
    tiles_per_run = RUN // KEY_TILE
    scale = HD ** (-0.5) * LOG2E

    def run_copy(run):
        layer, half = run // 2, run % 2
        return pltpu.make_async_copy(
            kv_hbm.at[pl.ds(half * PLANE, PLANE), layer], kv.at[run], sems.at[run]
        )

    for run in range(2 * LAYERS):
        run_copy(run).start()

    ones = jnp.ones((KEY_TILE, HD), jnp.bfloat16)

    def segment(j, _):
        base = (j * 2 + core) * RUN + slot * SEG
        run_copy(2 * j).wait()
        run_copy(2 * j + 1).wait()

        rows = base + lax.broadcasted_iota(jnp.int32, (SEG, 1), 0)
        first_doc = jnp.int32(0)
        last_doc = jnp.int32(0)
        row_doc = jnp.zeros((SEG, 1), jnp.int32)
        bound = jnp.int32(0)
        for d in range(ndoc):
            bound = bound + lengths[d]
            first_doc = jnp.where(bound <= base, bound, first_doc)
            last_doc = jnp.where(bound <= base + SEG - 1, bound, last_doc)
            row_doc = jnp.where(bound <= rows, bound, row_doc)

        acc[...] = jnp.zeros_like(acc)
        top[...] = jnp.full_like(top, NEG)

        def tile(t, masked):
            run = t // tiles_per_run
            part = t % tiles_per_run
            per = KEY_TILE // SEG
            block = kv[run, pl.ds(part * per, per)].reshape(KEY_TILE, 2 * HD)
            keys = block[:, :HD]
            values = jnp.concatenate([block[:, HD:], ones], axis=1)
            if masked:
                cols = t * KEY_TILE + lax.broadcasted_iota(jnp.int32, (1, KEY_TILE), 1)
                visible = (cols <= rows) & (cols >= row_doc)
            for h in range(GROUPS):
                query = q_ref[j, :, h * HD : (h + 1) * HD]
                scores = lax.dot_general(
                    query, keys, (((1,), (1,)), ((), ())), preferred_element_type=jnp.float32
                )
                if masked:
                    scores = jnp.where(visible, scores, NEG)
                old = top[h]
                new = jnp.maximum(old, jnp.max(scores, axis=1, keepdims=True) * scale)
                probs = jnp.exp2(scores * scale - new[:, :1]).astype(jnp.bfloat16)
                factor = jnp.exp2(old - new)
                product = jnp.dot(probs, values, preferred_element_type=jnp.float32)
                acc[h] = acc[h] * jnp.concatenate([factor, factor], axis=1) + product
                top[h] = new

        lo = first_doc // KEY_TILE
        diag = base // KEY_TILE
        full = jnp.minimum((last_doc + KEY_TILE - 1) // KEY_TILE, diag)

        def masked_tile(t, c):
            tile(t, True)
            return c

        def plain_tile(t, c):
            tile(t, False)
            return c

        lax.fori_loop(lo, full, masked_tile, 0)
        lax.fori_loop(full, diag, plain_tile, 0)
        tile(diag, True)

        for h in range(GROUPS):
            both = acc[h]
            attended = (both[:, :HD] / both[:, HD:]).astype(jnp.bfloat16)
            steer = steer_ref[:, h * HD : (h + 1) * HD]
            o_ref[j, :, h * HD : (h + 1) * HD] = (
                attended.astype(jnp.float32) + steer
            ).astype(jnp.bfloat16)
        return 0

    lax.fori_loop(0, LAYERS, segment, 0)


def attend(place, lengths, queries, gathered, steer):
    width = GROUPS * HD
    return pl.pallas_call(
        attend_kernel,
        out_shape=jax.ShapeDtypeStruct((LAYERS, SEG, width), jnp.bfloat16),
        in_specs=[
            pl.BlockSpec(memory_space=pltpu.SMEM),
            pl.BlockSpec(memory_space=pltpu.SMEM),
            pl.BlockSpec(memory_space=pltpu.VMEM),
            pl.BlockSpec(memory_space=pl.ANY),
            pl.BlockSpec(memory_space=pltpu.VMEM),
        ],
        out_specs=pl.BlockSpec(memory_space=pltpu.VMEM),
        scratch_shapes=[
            pltpu.VMEM((2 * LAYERS, PLANE, SEG, 2 * HD), jnp.bfloat16),
            pltpu.VMEM((GROUPS, SEG, 2 * HD), jnp.float32),
            pltpu.VMEM((GROUPS, SEG, HD), jnp.float32),
            pltpu.SemaphoreType.DMA((2 * LAYERS,)),
        ],
        compiler_params=pltpu.CompilerParams(vmem_limit_bytes=48 << 20),
        name="attend",
    )(place, lengths, queries, gathered, steer)


def body(queries, keys, values, doc_lengths, steering):
    tok = queries.shape[0]
    width = GROUPS * HD
    paired = jnp.concatenate(
        (keys.reshape(tok, KVH, HD), values.reshape(tok, KVH, HD)), axis=2
    ).transpose(1, 0, 2)
    kv_local = lax.all_to_all(paired, "z", 0, 0, tiled=True)
    gathered = lax.all_gather(kv_local, ("core", "y", "x"), axis=0, tiled=False)
    wide = queries.reshape(tok, KVH, width).transpose(1, 0, 2)
    wide, kv_local = lax.optimization_barrier((wide, kv_local))
    q_local = lax.all_to_all(wide, "z", 0, 0, tiled=True)
    place = jnp.stack(
        (lax.axis_index("core"), lax.axis_index("y") * 2 + lax.axis_index("x"))
    ).astype(jnp.int32)
    steer = lax.dynamic_slice_in_dim(steering, lax.axis_index("z") * width, width, 0)
    attended = attend(place, doc_lengths, q_local, gathered, steer[None, :])
    back = lax.all_to_all(attended, "z", 0, 0, tiled=True)
    return back.transpose(1, 0, 2).reshape(tok, KVH * width)


def solution(mesh):
    cells = Mesh(
        mesh.devices.reshape(LAYERS, 2, 4, 2, 2), ("z", "core", "y", "x", "dp")
    )
    tokens = P(("dp", "z", "core", "y", "x"), None)
    return jax.shard_map(
        body,
        mesh=cells,
        in_specs=(tokens, tokens, tokens, P("dp"), P()),
        out_specs=tokens,
        check_vma=False,
    )
```

```python
import jax
import jax.numpy as jnp
from jax import lax
from jax.experimental import pallas as pl
from jax.experimental.pallas import tpu as pltpu
from jax.sharding import Mesh
from jax.sharding import PartitionSpec as P

QH = 40
KVH = 8
HD = 128
GROUPS = QH // KVH
WIDTH = GROUPS * HD
NEG = -1e30
LOG2E = 1.4426950408889634
LAYERS = 8
PLANE = 8
SEG = 128
RUN = PLANE * SEG
BLOCKS = 2 * LAYERS * PLANE
ROWS = GROUPS * SEG
PER_TILE = 4
TILE = PER_TILE * SEG
UNROLL = 2
LIMIT = 100.0
PLACES = ((0, 0), (0, 1), (-1, 0), (1, 0), (-1, 1), (1, 1), (2, 0), (2, 1))


EVEN = (4, 2, 6, 0)
ODD = (3, 5, 1, 7)
TURNS = 4


def attend_kernel(place, turns, lengths, q_ref, *refs):
    pieces = refs[:16]
    steer_ref = refs[16]
    number = TURNS
    outs = refs[17 : 17 + number]
    kv, acc, top, qs, high, result, sems = refs[17 + number :]
    ndoc = lengths.shape[0]
    core, row, column, parity = place[0], place[1], place[2], place[3]
    slot = row * 2 + column
    scale = HD ** (-0.5) * LOG2E

    def copies(turn):
        out = []
        for side in range(2):
            for k, (dy, dx) in enumerate(PLACES):
                at_core = (core + side) % 2
                at_slot = ((row + dy + 4) % 4) * 2 + (column + dx) % 2
                n = side * 8 + k
                out.append(
                    pltpu.make_async_copy(
                        pieces[n].at[pl.ds(turn * 2, 2)],
                        kv.at[pl.ds(turn * 2, 2), at_core * PLANE + at_slot],
                        sems.at[turn, n],
                    )
                )
        return out

    for copy in copies(0):
        copy.start()
    ones = jnp.ones((TILE, HD), jnp.bfloat16)

    def wide(x, n):
        return jnp.concatenate([x] * (n // HD), axis=1)

    def segment(turn, _):
        @pl.when(turn + 1 < TURNS)
        def _():
            for copy in copies(turn + 1):
                copy.start()

        j = turn * 2 + parity
        base = (j * 2 + core) * RUN + slot * SEG
        rows = base + lax.broadcasted_iota(jnp.int32, (SEG, 1), 0)
        first = jnp.int32(0)
        row_doc = jnp.zeros((SEG, 1), jnp.int32)
        bound = jnp.int32(0)
        for d in range(ndoc):
            bound = bound + lengths[d]
            first = jnp.where(bound <= base, bound, first)
            row_doc = jnp.where(bound <= rows, bound, row_doc)
        low = first // SEG
        diag = base // SEG
        count = (diag + 1 - low + PER_TILE - 1) // PER_TILE

        for h in range(GROUPS):
            exact = q_ref[j, :, h * HD : (h + 1) * HD].astype(jnp.float32) * scale
            upper = exact.astype(jnp.bfloat16)
            qs[h * SEG : (h + 1) * SEG, :HD] = upper
            qs[h * SEG : (h + 1) * SEG, HD:] = (exact - upper.astype(jnp.float32)).astype(
                jnp.bfloat16
            )

        for copy in copies(turn):
            copy.wait()

        def scores(b, n):
            keys = jnp.concatenate(
                [kv[(b + u) // 16, (b + u) % 16, :HD, :] for u in range(n)], axis=1
            )
            return jnp.dot(
                qs[...],
                jnp.concatenate([keys, keys], axis=0),
                preferred_element_type=jnp.float32,
            )

        def hide(s, b, n, to_key):
            cols = b * SEG + lax.broadcasted_iota(jnp.int32, (1, n * SEG), 1)
            visible = (cols <= jnp.minimum(rows, to_key - 1)) & (cols >= row_doc)
            return jnp.where(
                visible[None], s.reshape(GROUPS, SEG, n * SEG), NEG
            ).reshape(ROWS, n * SEG)

        def tile_at(i):
            end = diag + 1 - i * PER_TILE
            b = jnp.maximum(end - PER_TILE, 0)
            rows_of = jnp.concatenate(
                [kv[(b + u) // 16, (b + u) % 16, HD:, :] for u in range(PER_TILE)], axis=0
            )
            return end * SEG, b, jnp.concatenate([rows_of, ones], axis=1)

        seed = jnp.maximum(diag - 1, 0)
        near = hide(scores(seed, 2), seed, 2, BLOCKS * SEG)
        top[...] = jnp.broadcast_to(jnp.max(near, axis=1, keepdims=True), (ROWS, HD))
        acc[...] = jnp.zeros_like(acc)
        high[...] = jnp.full_like(high, NEG)

        def tile(i):
            to_key, b, values = tile_at(i)
            x = hide(scores(b, PER_TILE) - wide(top[...], TILE), b, PER_TILE, to_key)
            peak = x[:, :HD]
            for u in range(1, PER_TILE):
                peak = jnp.maximum(peak, x[:, u * HD : (u + 1) * HD])
            high[...] = jnp.maximum(
                high[...], jnp.max(peak.reshape(ROWS // 8, 8, HD), axis=0)
            )
            probs = jnp.exp2(x).astype(jnp.bfloat16)
            acc[...] += jnp.dot(probs, values, preferred_element_type=jnp.float32)

        def group(g, c):
            for u in range(UNROLL):
                tile(g * UNROLL + u)
            return c

        def single(i, c):
            tile(i)
            return c

        lax.fori_loop(0, count // UNROLL, group, 0)
        lax.fori_loop((count // UNROLL) * UNROLL, count, single, 0)

        @pl.when(jnp.max(high[...]) > LIMIT)
        def _():
            acc[...] = jnp.zeros_like(acc)

            def again(i, c):
                to_key, b, values = tile_at(i)
                s = hide(scores(b, PER_TILE), b, PER_TILE, to_key)
                old = top[...]
                new = jnp.maximum(old, jnp.max(s, axis=1, keepdims=True))
                factor = jnp.exp2(old - new)
                probs = jnp.exp2(s - wide(new, TILE)).astype(jnp.bfloat16)
                acc[...] = acc[...] * wide(factor, 2 * HD) + jnp.dot(
                    probs, values, preferred_element_type=jnp.float32
                )
                top[...] = new
                return c

            lax.fori_loop(0, count, again, 0)

        for h in range(GROUPS):
            both = acc[h * SEG : (h + 1) * SEG]
            attended = (both[:, :HD] / both[:, HD:]).astype(jnp.bfloat16)
            steer = steer_ref[:, h * HD : (h + 1) * HD]
            result[turn, :, h * HD : (h + 1) * HD] = (
                attended.astype(jnp.float32) + steer
            ).astype(jnp.bfloat16)
        return 0

    lax.fori_loop(0, TURNS, segment, 0)
    for n in range(number):
        outs[n][...] = result[turns[n]]


def attend(place, turns, lengths, queries, pieces, steer):
    smem = pl.BlockSpec(memory_space=pltpu.SMEM)
    vmem = pl.BlockSpec(memory_space=pltpu.VMEM)
    hbm = pl.BlockSpec(memory_space=pltpu.HBM)
    f32, bf16 = jnp.float32, jnp.bfloat16
    number = TURNS
    return pl.pallas_call(
        attend_kernel,
        out_shape=[jax.ShapeDtypeStruct((SEG, WIDTH), bf16)] * number,
        in_specs=[smem, smem, smem, vmem] + [hbm] * 16 + [vmem],
        out_specs=[vmem] * number,
        scratch_shapes=[
            pltpu.VMEM((LAYERS, 2 * PLANE, 2 * HD, SEG), bf16),
            pltpu.VMEM((ROWS, 2 * HD), f32),
            pltpu.VMEM((ROWS, HD), f32),
            pltpu.VMEM((ROWS, 2 * HD), bf16),
            pltpu.VMEM((8, HD), f32),
            pltpu.VMEM((number, SEG, WIDTH), bf16),
            pltpu.SemaphoreType.DMA((TURNS, 16)),
        ],
        compiler_params=pltpu.CompilerParams(vmem_limit_bytes=20 << 20),
        cost_estimate=pl.CostEstimate(
            flops=number * ROWS * 3072 * 8 * HD,
            transcendentals=number * ROWS * 3072,
            bytes_accessed=BLOCKS * 4 * HD * SEG,
        ),
        name="attend",
    )(place, turns, lengths, queries, *pieces, steer)


def assemble_kernel(columns, *refs):
    parts, out = refs[:LAYERS], refs[LAYERS]
    for n in range(LAYERS):
        out[:, pl.ds(pl.multiple_of(columns[n] * WIDTH, HD), WIDTH)] = parts[n][...]


def assemble(columns, parts):
    smem = pl.BlockSpec(memory_space=pltpu.SMEM)
    vmem = pl.BlockSpec(memory_space=pltpu.VMEM)
    return pl.pallas_call(
        assemble_kernel,
        out_shape=jax.ShapeDtypeStruct((SEG, LAYERS * WIDTH), jnp.bfloat16),
        in_specs=[smem] + [vmem] * LAYERS,
        out_specs=vmem,
        name="assemble",
    )(columns, *parts)


def ring(own):
    flip = [(0, 1), (1, 0)]
    up = [(i, (i + 1) % 4) for i in range(4)]
    down = [(i, (i - 1) % 4) for i in range(4)]
    beside = lax.ppermute(own, "x", flip)
    up0 = lax.ppermute(own, "y", up)
    down0 = lax.ppermute(own, "y", down)
    up1 = lax.ppermute(beside, "y", up)
    down1 = lax.ppermute(beside, "y", down)
    far0 = lax.ppermute(up0, "y", up)
    far1 = lax.ppermute(down1, "y", down)
    mine = [own, beside, up0, down0, up1, down1, far0, far1]
    every = mine + [lax.ppermute(b, "core", flip) for b in mine]
    return [pltpu.with_memory_space_constraint(b, pltpu.HBM) for b in every]


def body(queries, keys, values, doc_lengths, steering):
    tok = queries.shape[0]
    paired = jnp.concatenate(
        (
            keys.reshape(tok, KVH, HD).transpose(1, 2, 0),
            values.reshape(tok, KVH, HD).transpose(1, 0, 2),
        ),
        axis=1,
    )
    kv_local = lax.all_to_all(paired, "z", 0, 0, tiled=True)
    large = queries.reshape(tok, KVH, WIDTH).transpose(1, 0, 2)
    large, kv_local = lax.optimization_barrier((large, kv_local))
    q_local = lax.all_to_all(large, "z", 0, 0, tiled=True)
    pieces = ring(kv_local)
    layer = lax.axis_index("z")

    def place(parity):
        return jnp.stack(
            (lax.axis_index("core"), lax.axis_index("y"), lax.axis_index("x"), parity)
        ).astype(jnp.int32)

    steer = lax.dynamic_slice_in_dim(steering, lax.axis_index("z") * WIDTH, WIDTH, 0)
    def send(part, shift):
        if shift == 0:
            return part
        return lax.ppermute(part, "z", [(i, (i + shift) % LAYERS) for i in range(LAYERS)])

    def run(flip, shifts, q):
        turns = (layer + jnp.array(shifts, jnp.int32)) % LAYERS // 2
        return attend(
            place((layer + flip) % 2), turns, doc_lengths, q, pieces, steer[None, :]
        )

    even = run(0, EVEN, q_local)
    sent = [send(p, s) for p, s in zip(even, EVEN)]
    q_again, _ = lax.optimization_barrier((q_local, tuple(even)))
    odd = run(1, ODD, q_again)
    odd, sent = lax.optimization_barrier((tuple(odd), tuple(sent)))
    sent = list(sent) + [send(p, s) for p, s in zip(odd, ODD)]
    columns = (layer - jnp.array(EVEN + ODD, jnp.int32) + LAYERS) % LAYERS
    return assemble(columns, sent)


def solution(mesh):
    cells = Mesh(
        mesh.devices.reshape(LAYERS, 2, 4, 2, 2), ("z", "core", "y", "x", "dp")
    )
    tokens = P(("dp", "z", "core", "y", "x"), None)
    return jax.shard_map(
        body,
        mesh=cells,
        in_specs=(tokens, tokens, tokens, P("dp"), P()),
        out_specs=tokens,
        check_vma=False,
    )
```

```python
import jax
import jax.numpy as jnp
from jax import lax
from jax.experimental import pallas as pl
from jax.experimental.pallas import tpu as pltpu
from jax.sharding import Mesh
from jax.sharding import PartitionSpec as P

QH = 40
KVH = 8
HD = 128
GROUPS = QH // KVH
WIDTH = GROUPS * HD
NEG = -1e30
LOG2E = 1.4426950408889634
LAYERS = 8
PLANE = 8
SEG = 128
RUN = PLANE * SEG
BLOCKS = 2 * LAYERS * PLANE
ROWS = GROUPS * SEG
PER_TILE = 4
TILE = PER_TILE * SEG
UNROLL = 2
LIMIT = 100.0
PLACES = ((0, 0), (0, 1), (-1, 0), (1, 0), (-1, 1), (1, 1), (2, 0), (2, 1))
PIECES = 2 * len(PLACES)


EVEN = (4, 2, 6, 0)
ODD = (3, 5, 1, 7)
TURNS = 4


def attend_kernel(place, turns, lengths, q_ref, *refs):
    pieces = refs[:PIECES]
    steer_ref = refs[PIECES]
    number = TURNS
    outs = refs[PIECES + 1 : PIECES + 1 + number]
    kv, acc, top, qs, high, result, sems = refs[PIECES + 1 + number :]
    ndoc = lengths.shape[0]
    core, row, column, parity = place[0], place[1], place[2], place[3]
    slot = row * 2 + column
    scale = HD ** (-0.5) * LOG2E

    def copies(turn):
        out = []
        for side in range(2):
            for k, (dy, dx) in enumerate(PLACES):
                at_core = (core + side) % 2
                at_slot = ((row + dy + 4) % 4) * 2 + (column + dx) % 2
                n = side * len(PLACES) + k
                out.append(
                    pltpu.make_async_copy(
                        pieces[n].at[pl.ds(turn * 2, 2)],
                        kv.at[pl.ds(turn * 2, 2), at_core * PLANE + at_slot],
                        sems.at[turn, n],
                    )
                )
        return out

    for copy in copies(0):
        copy.start()
    ones = jnp.ones((TILE, HD), jnp.bfloat16)

    def wide(x, n):
        return jnp.concatenate([x] * (n // HD), axis=1)

    def segment(turn, _):
        @pl.when(turn + 1 < TURNS)
        def _():
            for copy in copies(turn + 1):
                copy.start()

        j = turn * 2 + parity
        base = (j * 2 + core) * RUN + slot * SEG
        rows = base + lax.broadcasted_iota(jnp.int32, (SEG, 1), 0)
        first = jnp.int32(0)
        row_doc = jnp.zeros((SEG, 1), jnp.int32)
        bound = jnp.int32(0)
        for d in range(ndoc):
            bound = bound + lengths[d]
            first = jnp.where(bound <= base, bound, first)
            row_doc = jnp.where(bound <= rows, bound, row_doc)
        low = first // SEG
        diag = base // SEG
        count = (diag + 1 - low + PER_TILE - 1) // PER_TILE

        for h in range(GROUPS):
            exact = q_ref[j, :, h * HD : (h + 1) * HD].astype(jnp.float32) * scale
            upper = exact.astype(jnp.bfloat16)
            qs[h * SEG : (h + 1) * SEG, :HD] = upper
            qs[h * SEG : (h + 1) * SEG, HD:] = (exact - upper.astype(jnp.float32)).astype(
                jnp.bfloat16
            )

        for copy in copies(turn):
            copy.wait()

        def scores(b, n):
            keys = jnp.concatenate(
                [kv[(b + u) // 16, (b + u) % 16, :HD, :] for u in range(n)], axis=1
            )
            return jnp.dot(
                qs[...],
                jnp.concatenate([keys, keys], axis=0),
                preferred_element_type=jnp.float32,
            )

        def hide(s, b, n, to_key):
            cols = b * SEG + lax.broadcasted_iota(jnp.int32, (1, n * SEG), 1)
            visible = (cols <= jnp.minimum(rows, to_key - 1)) & (cols >= row_doc)
            return jnp.where(
                visible[None], s.reshape(GROUPS, SEG, n * SEG), NEG
            ).reshape(ROWS, n * SEG)

        def tile_at(i):
            end = diag + 1 - i * PER_TILE
            b = jnp.maximum(end - PER_TILE, 0)
            rows_of = jnp.concatenate(
                [kv[(b + u) // 16, (b + u) % 16, HD:, :] for u in range(PER_TILE)], axis=0
            )
            return end * SEG, b, jnp.concatenate([rows_of, ones], axis=1)

        seed = jnp.maximum(diag - 1, 0)
        near = hide(scores(seed, 2), seed, 2, BLOCKS * SEG)
        top[...] = jnp.broadcast_to(jnp.max(near, axis=1, keepdims=True), (ROWS, HD))
        acc[...] = jnp.zeros_like(acc)
        high[...] = jnp.full_like(high, NEG)

        def tile(i):
            to_key, b, values = tile_at(i)
            x = hide(scores(b, PER_TILE) - wide(top[...], TILE), b, PER_TILE, to_key)
            peak = x[:, :HD]
            for u in range(1, PER_TILE):
                peak = jnp.maximum(peak, x[:, u * HD : (u + 1) * HD])
            high[...] = jnp.maximum(
                high[...], jnp.max(peak.reshape(ROWS // 8, 8, HD), axis=0)
            )
            probs = jnp.exp2(x).astype(jnp.bfloat16)
            acc[...] += jnp.dot(probs, values, preferred_element_type=jnp.float32)

        def group(g, c):
            for u in range(UNROLL):
                tile(g * UNROLL + u)
            return c

        def single(i, c):
            tile(i)
            return c

        lax.fori_loop(0, count // UNROLL, group, 0)
        lax.fori_loop((count // UNROLL) * UNROLL, count, single, 0)

        @pl.when(jnp.max(high[...]) > LIMIT)
        def _():
            acc[...] = jnp.zeros_like(acc)

            def again(i, c):
                to_key, b, values = tile_at(i)
                s = hide(scores(b, PER_TILE), b, PER_TILE, to_key)
                old = top[...]
                new = jnp.maximum(old, jnp.max(s, axis=1, keepdims=True))
                factor = jnp.exp2(old - new)
                probs = jnp.exp2(s - wide(new, TILE)).astype(jnp.bfloat16)
                acc[...] = acc[...] * wide(factor, 2 * HD) + jnp.dot(
                    probs, values, preferred_element_type=jnp.float32
                )
                top[...] = new
                return c

            lax.fori_loop(0, count, again, 0)

        for h in range(GROUPS):
            both = acc[h * SEG : (h + 1) * SEG]
            attended = (both[:, :HD] / both[:, HD:]).astype(jnp.bfloat16)
            steer = steer_ref[:, h * HD : (h + 1) * HD]
            result[turn, :, h * HD : (h + 1) * HD] = (
                attended.astype(jnp.float32) + steer
            ).astype(jnp.bfloat16)
        return 0

    lax.fori_loop(0, TURNS, segment, 0)
    for n in range(number):
        outs[n][...] = result[turns[n]]


def attend(place, turns, lengths, queries, pieces, steer):
    smem = pl.BlockSpec(memory_space=pltpu.SMEM)
    vmem = pl.BlockSpec(memory_space=pltpu.VMEM)
    hbm = pl.BlockSpec(memory_space=pltpu.HBM)
    f32, bf16 = jnp.float32, jnp.bfloat16
    number = TURNS
    return pl.pallas_call(
        attend_kernel,
        out_shape=[jax.ShapeDtypeStruct((SEG, WIDTH), bf16)] * number,
        in_specs=[smem, smem, smem, vmem] + [hbm] * PIECES + [vmem],
        out_specs=[vmem] * number,
        scratch_shapes=[
            pltpu.VMEM((LAYERS, 2 * PLANE, 2 * HD, SEG), bf16),
            pltpu.VMEM((ROWS, 2 * HD), f32),
            pltpu.VMEM((ROWS, HD), f32),
            pltpu.VMEM((ROWS, 2 * HD), bf16),
            pltpu.VMEM((8, HD), f32),
            pltpu.VMEM((number, SEG, WIDTH), bf16),
            pltpu.SemaphoreType.DMA((TURNS, PIECES)),
        ],
        compiler_params=pltpu.CompilerParams(vmem_limit_bytes=20 << 20),
        cost_estimate=pl.CostEstimate(
            flops=number * ROWS * 3072 * 8 * HD,
            transcendentals=number * ROWS * 3072,
            bytes_accessed=BLOCKS * 4 * HD * SEG,
        ),
        name="attend",
    )(place, turns, lengths, queries, *pieces, steer)


def assemble_kernel(columns, *refs):
    parts, out = refs[:LAYERS], refs[LAYERS]
    for n in range(LAYERS):
        out[:, pl.ds(pl.multiple_of(columns[n] * WIDTH, HD), WIDTH)] = parts[n][...]


def assemble(columns, parts):
    smem = pl.BlockSpec(memory_space=pltpu.SMEM)
    vmem = pl.BlockSpec(memory_space=pltpu.VMEM)
    return pl.pallas_call(
        assemble_kernel,
        out_shape=jax.ShapeDtypeStruct((SEG, LAYERS * WIDTH), jnp.bfloat16),
        in_specs=[smem] + [vmem] * LAYERS,
        out_specs=vmem,
        name="assemble",
    )(columns, *parts)


def ring(own):
    flip = [(0, 1), (1, 0)]
    up = [(i, (i + 1) % 4) for i in range(4)]
    down = [(i, (i - 1) % 4) for i in range(4)]
    beside = lax.ppermute(own, "x", flip)
    up0 = lax.ppermute(own, "y", up)
    down0 = lax.ppermute(own, "y", down)
    beside, up0, down0 = lax.optimization_barrier((beside, up0, down0))
    far_keys = lax.ppermute(up0[:, :HD], "y", up)
    far_values = lax.ppermute(down0[:, HD:], "y", down)
    up1 = lax.ppermute(beside, "y", up)
    down1 = lax.ppermute(beside, "y", down)
    far0 = jnp.concatenate((far_keys, far_values), axis=1)
    far1 = lax.ppermute(far0, "x", flip)
    mine = [own, beside, up0, down0, up1, down1, far0, far1]
    every = mine + [lax.ppermute(b, "core", flip) for b in mine]
    return [pltpu.with_memory_space_constraint(b, pltpu.HBM) for b in every]


def pair_kernel(keys, values, out):
    for h in range(KVH):
        at = slice(h * HD, (h + 1) * HD)
        out[h, :HD, :] = keys[:, at].T
        out[h, HD:, :] = values[:, at]


def body(queries, keys, values, doc_lengths, steering):
    tok = queries.shape[0]
    paired = pl.pallas_call(
        pair_kernel,
        out_shape=jax.ShapeDtypeStruct((KVH, 2 * HD, tok), keys.dtype),
        name="pair",
    )(keys, values)
    kv_local = lax.all_to_all(paired, "z", 0, 0, tiled=True)
    large = queries.reshape(tok, KVH, WIDTH).transpose(1, 0, 2)
    large, kv_local = lax.optimization_barrier((large, kv_local))
    q_local = lax.all_to_all(large, "z", 0, 0, tiled=True)
    pieces = ring(kv_local)
    layer = lax.axis_index("z")

    def place(parity):
        return jnp.stack(
            (lax.axis_index("core"), lax.axis_index("y"), lax.axis_index("x"), parity)
        ).astype(jnp.int32)

    steer = lax.dynamic_slice_in_dim(steering, lax.axis_index("z") * WIDTH, WIDTH, 0)
    def send(part, shift):
        if shift == 0:
            return part
        return lax.ppermute(part, "z", [(i, (i + shift) % LAYERS) for i in range(LAYERS)])

    def run(flip, shifts, q):
        turns = (layer + jnp.array(shifts, jnp.int32)) % LAYERS // 2
        return attend(
            place((layer + flip) % 2), turns, doc_lengths, q, pieces, steer[None, :]
        )

    even = run(0, EVEN, q_local)
    sent = [send(p, s) for p, s in zip(even, EVEN)]
    q_again, _ = lax.optimization_barrier((q_local, tuple(even)))
    odd = run(1, ODD, q_again)
    odd, sent = lax.optimization_barrier((tuple(odd), tuple(sent)))
    sent = list(sent) + [send(p, s) for p, s in zip(odd, ODD)]
    columns = (layer - jnp.array(EVEN + ODD, jnp.int32) + LAYERS) % LAYERS
    return assemble(columns, sent)


def solution(mesh):
    cells = Mesh(
        mesh.devices.reshape(LAYERS, 2, 4, 2, 2), ("z", "core", "y", "x", "dp")
    )
    tokens = P(("dp", "z", "core", "y", "x"), None)
    return jax.shard_map(
        body,
        mesh=cells,
        in_specs=(tokens, tokens, tokens, P("dp"), P()),
        out_specs=tokens,
        check_vma=False,
    )
```

```python
import jax
import jax.numpy as jnp
from jax import lax
from jax.experimental import pallas as pl
from jax.experimental.pallas import tpu as pltpu
from jax.sharding import Mesh
from jax.sharding import PartitionSpec as P

QH = 40
KVH = 8
HD = 128
GROUPS = QH // KVH
WIDTH = GROUPS * HD
NEG = -1e30
LOG2E = 1.4426950408889634
LAYERS = 8
PLANE = 8
SEG = 128
RUN = PLANE * SEG
BLOCKS = 2 * LAYERS * PLANE
ROWS = GROUPS * SEG
PER_TILE = 4
TILE = PER_TILE * SEG
UNROLL = 3
LIMIT = 100.0
PLACES = ((0, 0), (0, 1), (-1, 0), (1, 0), (-1, 1), (1, 1), (2, 0), (2, 1))
PIECES = 2 * len(PLACES)


EVEN = (4, 2, 6, 0)
ODD = (3, 5, 1, 7)
TURNS = 4


def attend_kernel(place, turns, lengths, q_ref, *refs):
    pieces = refs[:PIECES]
    steer_ref = refs[PIECES]
    number = TURNS
    outs = refs[PIECES + 1 : PIECES + 1 + number]
    kv, acc, top, qs, high, result, sems = refs[PIECES + 1 + number :]
    ndoc = lengths.shape[0]
    core, row, column, parity = place[0], place[1], place[2], place[3]
    slot = row * 2 + column
    scale = HD ** (-0.5) * LOG2E

    def copies(turn):
        out = []
        for side in range(2):
            for k, (dy, dx) in enumerate(PLACES):
                at_core = (core + side) % 2
                at_slot = ((row + dy + 4) % 4) * 2 + (column + dx) % 2
                n = side * len(PLACES) + k
                out.append(
                    pltpu.make_async_copy(
                        pieces[n].at[pl.ds(turn * 2, 2)],
                        kv.at[pl.ds(turn * 2, 2), at_core * PLANE + at_slot],
                        sems.at[turn, n],
                    )
                )
        return out

    for copy in copies(0):
        copy.start()
    ones = jnp.ones((TILE, HD), jnp.bfloat16)

    def wide(x, n):
        return jnp.concatenate([x] * (n // HD), axis=1)

    def segment(turn, _):
        @pl.when(turn + 1 < TURNS)
        def _():
            for copy in copies(turn + 1):
                copy.start()

        j = turn * 2 + parity
        base = (j * 2 + core) * RUN + slot * SEG
        rows = base + lax.broadcasted_iota(jnp.int32, (SEG, 1), 0)
        first = jnp.int32(0)
        row_doc = jnp.zeros((SEG, 1), jnp.int32)
        bound = jnp.int32(0)
        for d in range(ndoc):
            bound = bound + lengths[d]
            first = jnp.where(bound <= base, bound, first)
            row_doc = jnp.where(bound <= rows, bound, row_doc)
        low = first // SEG
        diag = base // SEG
        count = (diag + 1 - low + PER_TILE - 1) // PER_TILE

        for h in range(GROUPS):
            exact = q_ref[j, :, h * HD : (h + 1) * HD].astype(jnp.float32) * scale
            upper = exact.astype(jnp.bfloat16)
            qs[h * SEG : (h + 1) * SEG, :HD] = upper
            qs[h * SEG : (h + 1) * SEG, HD:] = (exact - upper.astype(jnp.float32)).astype(
                jnp.bfloat16
            )

        for copy in copies(turn):
            copy.wait()

        def scores(b, n):
            keys = jnp.concatenate(
                [kv[(b + u) // 16, (b + u) % 16, :HD, :] for u in range(n)], axis=1
            )
            return jnp.dot(
                qs[...],
                jnp.concatenate([keys, keys], axis=0),
                preferred_element_type=jnp.float32,
            )

        def hide(s, b, n, to_key):
            cols = b * SEG + lax.broadcasted_iota(jnp.int32, (1, n * SEG), 1)
            visible = (cols <= jnp.minimum(rows, to_key - 1)) & (cols >= row_doc)
            return jnp.where(
                visible[None], s.reshape(GROUPS, SEG, n * SEG), NEG
            ).reshape(ROWS, n * SEG)

        def tile_at(i):
            end = diag + 1 - i * PER_TILE
            b = jnp.maximum(end - PER_TILE, 0)
            rows_of = jnp.concatenate(
                [kv[(b + u) // 16, (b + u) % 16, HD:, :] for u in range(PER_TILE)], axis=0
            )
            return end * SEG, b, jnp.concatenate([rows_of, ones], axis=1)

        seed = jnp.maximum(diag - 1, 0)
        near = hide(scores(seed, 2), seed, 2, BLOCKS * SEG)
        top[...] = jnp.broadcast_to(jnp.max(near, axis=1, keepdims=True), (ROWS, HD))
        acc[...] = jnp.zeros_like(acc)
        high[...] = jnp.full_like(high, NEG)

        def tile(i):
            to_key, b, values = tile_at(i)
            x = hide(scores(b, PER_TILE) - wide(top[...], TILE), b, PER_TILE, to_key)
            peak = x[:, :HD]
            for u in range(1, PER_TILE):
                peak = jnp.maximum(peak, x[:, u * HD : (u + 1) * HD])
            high[...] = jnp.maximum(
                high[...], jnp.max(peak.reshape(ROWS // 8, 8, HD), axis=0)
            )
            probs = jnp.exp2(x).astype(jnp.bfloat16)
            acc[...] += jnp.dot(probs, values, preferred_element_type=jnp.float32)

        def group(g, c):
            for u in range(UNROLL):
                tile(g * UNROLL + u)
            return c

        def single(i, c):
            tile(i)
            return c

        lax.fori_loop(0, count // UNROLL, group, 0)
        lax.fori_loop((count // UNROLL) * UNROLL, count, single, 0)

        @pl.when(jnp.max(high[...]) > LIMIT)
        def _():
            acc[...] = jnp.zeros_like(acc)

            def again(i, c):
                to_key, b, values = tile_at(i)
                s = hide(scores(b, PER_TILE), b, PER_TILE, to_key)
                old = top[...]
                new = jnp.maximum(old, jnp.max(s, axis=1, keepdims=True))
                factor = jnp.exp2(old - new)
                probs = jnp.exp2(s - wide(new, TILE)).astype(jnp.bfloat16)
                acc[...] = acc[...] * wide(factor, 2 * HD) + jnp.dot(
                    probs, values, preferred_element_type=jnp.float32
                )
                top[...] = new
                return c

            lax.fori_loop(0, count, again, 0)

        for h in range(GROUPS):
            both = acc[h * SEG : (h + 1) * SEG]
            attended = (both[:, :HD] / both[:, HD:]).astype(jnp.bfloat16)
            steer = steer_ref[:, h * HD : (h + 1) * HD]
            result[turn, :, h * HD : (h + 1) * HD] = (
                attended.astype(jnp.float32) + steer
            ).astype(jnp.bfloat16)
        return 0

    lax.fori_loop(0, TURNS, segment, 0)
    for n in range(number):
        outs[n][...] = result[turns[n]]


def attend(place, turns, lengths, queries, pieces, steer):
    smem = pl.BlockSpec(memory_space=pltpu.SMEM)
    vmem = pl.BlockSpec(memory_space=pltpu.VMEM)
    hbm = pl.BlockSpec(memory_space=pltpu.HBM)
    f32, bf16 = jnp.float32, jnp.bfloat16
    number = TURNS
    return pl.pallas_call(
        attend_kernel,
        out_shape=[jax.ShapeDtypeStruct((SEG, WIDTH), bf16)] * number,
        in_specs=[smem, smem, smem, vmem] + [hbm] * PIECES + [vmem],
        out_specs=[vmem] * number,
        scratch_shapes=[
            pltpu.VMEM((LAYERS, 2 * PLANE, 2 * HD, SEG), bf16),
            pltpu.VMEM((ROWS, 2 * HD), f32),
            pltpu.VMEM((ROWS, HD), f32),
            pltpu.VMEM((ROWS, 2 * HD), bf16),
            pltpu.VMEM((8, HD), f32),
            pltpu.VMEM((number, SEG, WIDTH), bf16),
            pltpu.SemaphoreType.DMA((TURNS, PIECES)),
        ],
        compiler_params=pltpu.CompilerParams(vmem_limit_bytes=20 << 20),
        cost_estimate=pl.CostEstimate(
            flops=number * ROWS * 3072 * 8 * HD,
            transcendentals=number * ROWS * 3072,
            bytes_accessed=BLOCKS * 4 * HD * SEG,
        ),
        name="attend",
    )(place, turns, lengths, queries, *pieces, steer)


def assemble_kernel(columns, *refs):
    parts, out = refs[:LAYERS], refs[LAYERS]
    for n in range(LAYERS):
        out[:, pl.ds(pl.multiple_of(columns[n] * WIDTH, HD), WIDTH)] = parts[n][...]


def assemble(columns, parts):
    smem = pl.BlockSpec(memory_space=pltpu.SMEM)
    vmem = pl.BlockSpec(memory_space=pltpu.VMEM)
    return pl.pallas_call(
        assemble_kernel,
        out_shape=jax.ShapeDtypeStruct((SEG, LAYERS * WIDTH), jnp.bfloat16),
        in_specs=[smem] + [vmem] * LAYERS,
        out_specs=vmem,
        name="assemble",
    )(columns, *parts)


def ring(own):
    flip = [(0, 1), (1, 0)]
    up = [(i, (i + 1) % 4) for i in range(4)]
    down = [(i, (i - 1) % 4) for i in range(4)]
    beside = lax.ppermute(own, "x", flip)
    up0 = lax.ppermute(own, "y", up)
    down0 = lax.ppermute(own, "y", down)
    beside, up0, down0 = lax.optimization_barrier((beside, up0, down0))
    far_keys = lax.ppermute(up0[:, :HD], "y", up)
    far_values = lax.ppermute(down0[:, HD:], "y", down)
    up1 = lax.ppermute(beside, "y", up)
    down1 = lax.ppermute(beside, "y", down)
    far0 = jnp.concatenate((far_keys, far_values), axis=1)
    far1 = lax.ppermute(far0, "x", flip)
    mine = [own, beside, up0, down0, up1, down1, far0, far1]
    every = mine + [lax.ppermute(b, "core", flip) for b in mine]
    return [pltpu.with_memory_space_constraint(b, pltpu.HBM) for b in every]


def pair_kernel(keys, values, out):
    for h in range(KVH):
        at = slice(h * HD, (h + 1) * HD)
        out[h, :HD, :] = keys[:, at].T
        out[h, HD:, :] = values[:, at]


def body(queries, keys, values, doc_lengths, steering):
    tok = queries.shape[0]
    paired = pl.pallas_call(
        pair_kernel,
        out_shape=jax.ShapeDtypeStruct((KVH, 2 * HD, tok), keys.dtype),
        name="pair",
    )(keys, values)
    kv_local = lax.all_to_all(paired, "z", 0, 0, tiled=True)
    large = queries.reshape(tok, KVH, WIDTH).transpose(1, 0, 2)
    large, kv_local = lax.optimization_barrier((large, kv_local))
    q_local = lax.all_to_all(large, "z", 0, 0, tiled=True)
    pieces = ring(kv_local)
    layer = lax.axis_index("z")

    def place(parity):
        return jnp.stack(
            (lax.axis_index("core"), lax.axis_index("y"), lax.axis_index("x"), parity)
        ).astype(jnp.int32)

    steer = lax.dynamic_slice_in_dim(steering, lax.axis_index("z") * WIDTH, WIDTH, 0)
    def send(part, shift):
        if shift == 0:
            return part
        return lax.ppermute(part, "z", [(i, (i + shift) % LAYERS) for i in range(LAYERS)])

    def run(flip, shifts, q):
        turns = (layer + jnp.array(shifts, jnp.int32)) % LAYERS // 2
        return attend(
            place((layer + flip) % 2), turns, doc_lengths, q, pieces, steer[None, :]
        )

    even = run(0, EVEN, q_local)
    sent = [send(p, s) for p, s in zip(even, EVEN)]
    q_again, _ = lax.optimization_barrier((q_local, tuple(even)))
    odd = run(1, ODD, q_again)
    odd, sent = lax.optimization_barrier((tuple(odd), tuple(sent)))
    sent = list(sent) + [send(p, s) for p, s in zip(odd, ODD)]
    columns = (layer - jnp.array(EVEN + ODD, jnp.int32) + LAYERS) % LAYERS
    return assemble(columns, sent)


def solution(mesh):
    cells = Mesh(
        mesh.devices.reshape(LAYERS, 2, 4, 2, 2), ("z", "core", "y", "x", "dp")
    )
    tokens = P(("dp", "z", "core", "y", "x"), None)
    return jax.shard_map(
        body,
        mesh=cells,
        in_specs=(tokens, tokens, tokens, P("dp"), P()),
        out_specs=tokens,
        check_vma=False,
    )
```
